32 devices in a mesh: dp: 4 (over y, core), ctx: 8 (over z, x).
Axes of the slice: x: 2, y: 2, z: 4, core: 2. Of those that a mesh axis runs over, the one named last changes fastest.
Arguments:
- tokens: bfloat16 [4, 1024, 1024], P('dp', 'ctx'), may hold values from -6 to 6
- positions: int32 [4, 1024], P('dp', 'ctx'), may hold values from 0 to 1023, as said below
- d_out: bfloat16 [4, 1024, 1024], P('dp', 'ctx'), may hold values from -6 to 6
- first_gain: bfloat16 [1024], P(('dp', 'ctx')), may hold values from 0.099609375 to 1.8984375
- second_gain: bfloat16 [1024], P(('dp', 'ctx')), may hold values from 0.099609375 to 1.8984375
- query_gain: bfloat16 [64], replicated, may hold values from 0.5 to 4
- key_gain: bfloat16 [64], replicated, may hold values from 0.5 to 4
- query_weight: bfloat16 [1024, 1024], P(('dp', 'ctx')), may hold values from -0.1875 to 0.1875
- key_weight: bfloat16 [1024, 512], P(('dp', 'ctx')), may hold values from -0.1875 to 0.1875
- value_weight: bfloat16 [1024, 512], P(('dp', 'ctx')), may hold values from -0.1875 to 0.1875
- out_weight: bfloat16 [1024, 1024], P(('dp', 'ctx')), may hold values from -2 to 2
- gate_weight: bfloat16 [1024, 4608], P(('dp', 'ctx')), may hold values from -0.1875 to 0.1875
- up_weight: bfloat16 [1024, 4608], P(('dp', 'ctx')), may hold values from -0.1875 to 0.1875
- down_weight: bfloat16 [4608, 1024], P(('dp', 'ctx')), may hold values from -0.09375 to 0.09375
Outputs:
- output: bfloat16 [4, 1024, 1024], P('dp', 'ctx')
- d_tokens: float32 [4, 1024, 1024], P('dp', 'ctx')
- first_gain_grad: float32 [1024], P(('dp', 'ctx'))
- second_gain_grad: float32 [1024], P(('dp', 'ctx'))
- query_gain_grad: float32 [64], replicated
- key_gain_grad: float32 [64], replicated
- query_weight_grad: float32 [1024, 1024], P(('dp', 'ctx'))
- key_weight_grad: float32 [1024, 512], P(('dp', 'ctx'))
- value_weight_grad: float32 [1024, 512], P(('dp', 'ctx'))
- out_weight_grad: float32 [1024, 1024], P(('dp', 'ctx'))
- gate_weight_grad: float32 [1024, 4608], P(('dp', 'ctx'))
- up_weight_grad: float32 [1024, 4608], P(('dp', 'ctx'))
- down_weight_grad: float32 [4608, 1024], P(('dp', 'ctx'))
The draws below stay inside these ranges and needn't reach their ends.
Inputs may be any that keep to these rules, and one draw needn't show every extreme that they name: positions restart at 0 at the first token of each packed document and rise by one a token; every sequence begins with a document, and the first sequence is one document.
All inputs are finite; a program needn't handle non-finite values.
Results may differ from the reference program's by a relative error of at most 0.02.
The reference program's roundings to bfloat16 on the way count: a program that leaves them out, or rounds other values in their place, can miss the bound.
Values may be sent and summed in bfloat16 or wider, within the bound.
No kernel may reach another device: no remote copies, remote signals or barrier semaphores. Data moves between devices by JAX's collectives and lax.ppermute only.
A program may use at most 192 MiB of HBM per device.

```python
import jax
import jax.numpy as jnp
from jax import lax

D = 1024
H = 16
KV = 8
DH = 64
FF = 4608
LENGTH = 1024
SEQ_ALL = 4


def draw_positions(key, part):
    seeded = jax.random.fold_in(key, 13)
    starts = jax.random.randint(seeded, (SEQ_ALL, LENGTH), 0, LENGTH) < 4
    index_row = jnp.arange(LENGTH, dtype=jnp.int32)
    first_seq = (jnp.arange(SEQ_ALL, dtype=jnp.int32) == 0)[:, None]
    starts = jnp.logical_and(starts, jnp.logical_not(first_seq))
    starts = jnp.logical_or(starts, (index_row == 0)[None, :])
    latest = lax.cummax(jnp.where(starts, index_row[None, :], 0), axis=1)
    return (index_row[None, :] - latest).astype(jnp.int32)


def draw_query_gain(key, part):
    seeded = jax.random.fold_in(key, 11)
    return jnp.exp(jax.random.uniform(seeded, (DH,), jnp.float32, jnp.log(0.5), jnp.log(1.6))).astype(jnp.bfloat16)


def draw_key_gain(key, part):
    seeded = jax.random.fold_in(key, 12)
    return jnp.exp(jax.random.uniform(seeded, (DH,), jnp.float32, jnp.log(0.5), jnp.log(1.6))).astype(jnp.bfloat16)


def spiked(array, key, source, target, blocks, factor):
    owner, partner = [(jnp.arange(array.shape[position]) // (array.shape[position] // blocks)).reshape([-1 if axis == position else 1 for axis in range(array.ndim)]) for position in (source, target)]
    chosen = jax.random.permutation(key, blocks)[partner]
    strong = (owner == chosen) | (owner == (partner + blocks // 2) % blocks)
    return jnp.where(strong, factor * array, array)


def shard_levels(rng, shape, pieces, smallest, high):
    loudness, own = 1.0, jax.random.fold_in(rng, 6)
    for dim, parts in pieces:
        steps = jnp.exp(jax.random.uniform(jax.random.fold_in(own, dim), (parts,), jnp.float32, smallest / len(pieces), high / len(pieces)))
        loudness = loudness * jnp.repeat(steps, shape[dim] // parts).reshape([-1 if axis == dim else 1 for axis in range(len(shape))])
    return loudness


def normal_values(rng, shape, deviation, reach, cuts=(), held_as=jnp.bfloat16):
    values = jax.random.normal(rng, shape, jnp.float32) * deviation
    if len(cuts) > 0:
        values = shard_levels(rng, shape, cuts, -0.22, 0.18) * values
    return jnp.clip(values, min=-reach, max=reach).astype(held_as)


def gaussian_with(key, shape, scale, bound, cuts, heavy, held_as=jnp.bfloat16):
    drawn = scale * jax.random.normal(key, shape, jnp.float32)
    if cuts:
        drawn = drawn * shard_levels(key, shape, cuts, -0.22, 0.18)
    return jnp.clip(spiked(drawn, jax.random.fold_in(key, 3), *heavy), -bound, bound).astype(held_as)


def setup_inputs(seed: int = 0) -> dict:
    key_list = jax.random.split(jax.random.key(seed), 15)
    tokens = gaussian_with(key_list[0], (SEQ_ALL, LENGTH, D), 1.0, 6.0, ((0, 4), (1, 8)), (1, 2, 8, 2.0))
    positions = draw_positions(jax.random.fold_in(key_list[14], 71), 0)
    d_out = normal_values(key_list[2], (SEQ_ALL, LENGTH, D), 1.0, 6.0, ((0, 4), (1, 8)))
    first_gain = jnp.clip(1.0 + 0.18 * jax.random.normal(key_list[3], (D,), jnp.float32), 0.099609375, 1.8984375).astype(jnp.bfloat16)
    second_gain = jnp.clip(1.0 + 0.18 * jax.random.normal(key_list[4], (D,), jnp.float32), 0.099609375, 1.8984375).astype(jnp.bfloat16)
    query_gain = draw_query_gain(jax.random.fold_in(key_list[14], 71), 0)
    key_gain = draw_key_gain(jax.random.fold_in(key_list[14], 71), 0)
    query_weight = normal_values(key_list[7], (D, H * DH), D ** -0.5, 0.1875, ((0, 32),))
    key_weight = normal_values(key_list[8], (D, KV * DH), D ** -0.5, 0.1875, ((0, 32),))
    value_weight = normal_values(key_list[9], (D, KV * DH), D ** -0.5, 0.1875, ((0, 32),))
    out_weight = normal_values(key_list[10], (H * DH, D), (DH // 8) ** -0.5, 2.0, ((0, 32),))
    gate_weight = normal_values(key_list[11], (D, FF), D ** -0.5, 0.1875, ((0, 32),))
    up_weight = normal_values(key_list[12], (D, FF), D ** -0.5, 0.1875, ((0, 32),))
    down_weight = normal_values(key_list[13], (FF, D), FF ** -0.5, 0.09375, ((0, 32),))
    return {"tokens": tokens, "positions": positions, "d_out": d_out, "first_gain": first_gain, "second_gain": second_gain, "query_gain": query_gain, "key_gain": key_gain, "query_weight": query_weight, "key_weight": key_weight, "value_weight": value_weight, "out_weight": out_weight, "gate_weight": gate_weight, "up_weight": up_weight, "down_weight": down_weight}


epsilon = 1e-05
rope_base = 1000000.0
masked_value = -1e+30
highest = lax.Precision.HIGHEST

@jax.custom_vjp
def low(v):
    return lax.optimization_barrier(v.astype(jnp.bfloat16)).astype(jnp.float32)

@jax.custom_vjp
def low_back(v):
    return v

def low_keep(v):
    return (low(v), None)

def low_pass(kept, grad):
    return (grad,)

def back_keep(v):
    return (v, None)

def back_low(kept, grad):
    return (low(grad),)
low.defvjp(low_keep, low_pass)
low_back.defvjp(back_keep, back_low)

def norm_rows(values, gain_row):
    return values * lax.rsqrt(lax.optimization_barrier(jnp.mean(values * values, axis=-1, keepdims=True)) + epsilon) * gain_row

def rope_tables(seq_positions):
    frequency = rope_base ** (-jnp.arange(0, DH, 2, dtype=jnp.float32) / DH)
    angles = seq_positions.astype(jnp.float32)[..., None] * frequency
    return (jnp.cos(angles)[..., None, :], jnp.sin(angles)[..., None, :])

def rotate(values, cosine, sine_part):
    half_size = values.shape[-1] // 2
    half_one = values[..., :half_size]
    half_two = values[..., half_size:]
    return jnp.concatenate([half_one * cosine - half_two * sine_part, half_two * cosine + half_one * sine_part], axis=-1)

def block_forward(sequence, seq_positions, params):
    gain_first, gain_second, query_scale, key_scale, query_full, key_full, value_full, out_full, gate_full, up_full, down_full = params
    length = sequence.shape[0]
    group_ratio = H // KV
    score_scale = DH ** (-0.5)
    cosine, sine_part = rope_tables(seq_positions)
    normed_one = low(norm_rows(sequence, gain_first))
    query_raw = low_back(jnp.dot(normed_one, query_full, precision=highest)).reshape(length, H, DH)
    key_raw = low_back(jnp.dot(normed_one, key_full, precision=highest)).reshape(length, KV, DH)
    value_rows = low_back(low(jnp.dot(normed_one, value_full, precision=highest))).reshape(length, KV, DH)
    query_rot = low_back(low(rotate(norm_rows(query_raw, query_scale), cosine, sine_part)))
    key_rot = low_back(low(rotate(norm_rows(key_raw, key_scale), cosine, sine_part)))
    query_rows = min(512, length)
    query_blocks = query_rot.reshape(length // query_rows, query_rows, KV, group_ratio, DH)
    key_pos = jnp.arange(length).astype(jnp.int32)

    def attend(block_args):
        query_block, block_first = block_args
        scores = low_back(jnp.einsum('qgrd,kgd->grqk', query_block, key_rot, precision=highest) * score_scale)
        query_pos = block_first + jnp.arange(query_rows).astype(jnp.int32)
        causal = key_pos[None, :] <= query_pos[:, None]
        scores = jnp.where(causal, scores, masked_value)
        shifted = jnp.exp(scores - lax.optimization_barrier(jnp.max(scores, axis=-1, keepdims=True)))
        probabilities = low(shifted / lax.optimization_barrier(jnp.sum(shifted, axis=-1, keepdims=True)))
        mixed_rows = jnp.einsum('grqk,kgd->qgrd', probabilities, value_rows, precision=highest)
        return mixed_rows.reshape(query_rows, H * DH)
    firsts = (jnp.arange(length // query_rows) * query_rows).astype(jnp.int32)
    attn_rows = lax.map(jax.checkpoint(attend), (query_blocks, firsts))
    attn_rows = low_back(low(attn_rows.reshape(length, H * DH)))
    middle = sequence + low_back(jnp.dot(attn_rows, out_full, precision=highest))
    normed_two = low(norm_rows(middle, gain_second))
    gate_pre = low_back(jnp.dot(normed_two, gate_full, precision=highest))
    up_pre = low_back(jnp.dot(normed_two, up_full, precision=highest))
    hidden = low(jax.nn.silu(gate_pre) * up_pre)
    return middle + low_back(jnp.dot(hidden, down_full, precision=highest))

def reference(tokens, positions, d_out, first_gain, second_gain, query_gain, key_gain, query_weight, key_weight, value_weight, out_weight, gate_weight, up_weight, down_weight):
    params = tuple((argument.astype(jnp.float32) for argument in (first_gain, second_gain, query_gain, key_gain, query_weight, key_weight, value_weight, out_weight, gate_weight, up_weight, down_weight)))

    def one_sequence(totals, seq_item):
        sequence, seq_positions, cotangent = seq_item
        result, pullback = jax.vjp(lambda seq_rows, weights: block_forward(seq_rows, seq_positions, weights), sequence.astype(jnp.float32), params)
        grad_rows, grad_params = pullback(cotangent.astype(jnp.float32))
        return (jax.tree.map(jnp.add, totals, grad_params), (result.astype(jnp.bfloat16), grad_rows))
    zeros = tuple((jnp.zeros_like(argument) for argument in params))
    totals, (outputs, grad_tokens) = lax.scan(one_sequence, zeros, (tokens, positions, d_out))
    return (outputs, grad_tokens, totals[0], totals[1], totals[2], totals[3], totals[4], totals[5], totals[6], totals[7], totals[8], totals[9], totals[10])
```

```python
import jax
import jax.numpy as jnp
from jax import lax
from jax.experimental import pallas as pl
from jax.experimental.pallas import tpu as pltpu
from jax.sharding import Mesh, PartitionSpec as P

H = 16
KV = 8
DH = 64


epsilon = 1e-05
rope_base = 1000000.0
masked_value = -1e30


def norm_rows(values, gain_row):
    return (
        values * lax.rsqrt(jnp.mean(values * values, axis=-1, keepdims=True) + epsilon) * gain_row
    )


def norm_back(values, gain_row, grad_out):
    scale_rows = lax.rsqrt(jnp.mean(values * values, axis=-1, keepdims=True) + epsilon)
    normed = values * scale_rows
    grad_normed = grad_out * gain_row
    grad_in = scale_rows * (
        grad_normed - normed * jnp.mean(grad_normed * normed, axis=-1, keepdims=True)
    )
    return (grad_in, grad_out * normed)


def rope_tables(seq_positions):
    frequency = rope_base ** (-jnp.arange(0, DH, 2, dtype=jnp.float32) / DH)
    angles = seq_positions.astype(jnp.float32)[..., None] * frequency
    return (jnp.cos(angles)[..., None, :], jnp.sin(angles)[..., None, :])


def rotate(values, cosine, sine_part):
    half_size = values.shape[-1] // 2
    half_one = values[..., :half_size]
    half_two = values[..., half_size:]
    return jnp.concatenate(
        [half_one * cosine - half_two * sine_part, half_two * cosine + half_one * sine_part],
        axis=-1,
    )


def rotate_back(grads_in, cosine, sine_part):
    half_size = grads_in.shape[-1] // 2
    half_one = grads_in[..., :half_size]
    half_two = grads_in[..., half_size:]
    return jnp.concatenate(
        [half_one * cosine + half_two * sine_part, half_two * cosine - half_one * sine_part],
        axis=-1,
    )


def sum_rows(values):
    return jnp.sum(values.reshape(-1, values.shape[-1]), axis=0)


def row_product(left_rows, right_rows):
    return jnp.einsum("sba,sbc->ac", left_rows, right_rows, preferred_element_type=jnp.float32)


def rounded(values):
    return lax.optimization_barrier(values.astype(jnp.bfloat16)).astype(jnp.float32)


def generic_device(
    tokens,
    positions,
    d_out,
    first_gain,
    second_gain,
    query_gain,
    key_gain,
    query_weight,
    key_weight,
    value_weight,
    out_weight,
    gate_weight,
    up_weight,
    down_weight,
):
    num_seqs, blk_rows = (tokens.shape[0], tokens.shape[1])
    group_ratio = H // KV
    score_scale = DH ** (-0.5)
    shards = (
        first_gain,
        second_gain,
        query_weight,
        key_weight,
        value_weight,
        out_weight,
        gate_weight,
        up_weight,
        down_weight,
    )
    full_params = (
        lax.all_gather(shards[0], ("dp", "ctx"), axis=0, tiled=True),
        lax.all_gather(shards[1], ("dp", "ctx"), axis=0, tiled=True),
        lax.all_gather(shards[2], ("dp", "ctx"), axis=0, tiled=True),
        lax.all_gather(shards[3], ("dp", "ctx"), axis=0, tiled=True),
        lax.all_gather(shards[4], ("dp", "ctx"), axis=0, tiled=True),
        lax.all_gather(shards[5], ("dp", "ctx"), axis=0, tiled=True),
        lax.all_gather(shards[6], ("dp", "ctx"), axis=0, tiled=True),
        lax.all_gather(shards[7], ("dp", "ctx"), axis=0, tiled=True),
        lax.all_gather(shards[8], ("dp", "ctx"), axis=0, tiled=True),
    )
    (
        gain_first,
        gain_second,
        query_full,
        key_full,
        value_full,
        out_full,
        gate_full,
        up_full,
        down_full,
    ) = full_params
    query_scale = query_gain.astype(jnp.float32)
    key_scale = key_gain.astype(jnp.float32)
    input_rows = tokens.astype(jnp.float32)
    cosine, sine_part = rope_tables(positions)
    normed_one = norm_rows(input_rows, gain_first.astype(jnp.float32)).astype(jnp.bfloat16)
    query_raw = jnp.dot(normed_one, query_full, preferred_element_type=jnp.float32).reshape(
        num_seqs, blk_rows, H, DH
    )
    key_raw = jnp.dot(normed_one, key_full, preferred_element_type=jnp.float32).reshape(
        num_seqs, blk_rows, KV, DH
    )
    value_rows = jnp.dot(normed_one, value_full, preferred_element_type=jnp.float32).astype(
        jnp.bfloat16
    )
    query_rot = rotate(norm_rows(query_raw, query_scale), cosine, sine_part)
    key_rot = rotate(norm_rows(key_raw, key_scale), cosine, sine_part)
    query_bf = query_rot.astype(jnp.bfloat16).reshape(num_seqs, blk_rows, KV, group_ratio, DH)
    key_bf = key_rot.astype(jnp.bfloat16).reshape(num_seqs, blk_rows, KV * DH)
    own_index = lax.axis_index("ctx")
    query_base = own_index * blk_rows
    row_ids = jnp.arange(blk_rows, dtype=jnp.int32)
    query_pos = query_base + row_ids
    query_last = query_base + blk_rows - 1

    def causal_at(key_first):
        return (key_first + row_ids)[None, :] <= query_pos[:, None]

    stat_shape = (num_seqs, KV, group_ratio, blk_rows)
    init_fwd = (
        jnp.full(stat_shape, masked_value, jnp.float32),
        jnp.zeros(stat_shape, jnp.float32),
        jnp.zeros(stat_shape + (DH,), jnp.float32),
    )
    key_piece = lax.all_gather(key_bf, "ctx", axis=1, tiled=True)
    value_piece = lax.all_gather(value_rows, "ctx", axis=1, tiled=True)
    num_blocks = key_piece.shape[1] // blk_rows

    def one_block(block_index, running):
        kstart = block_index * blk_rows

        def compute(current):
            row_max, row_sum, weighted = current
            key_blk = lax.dynamic_slice_in_dim(
                key_piece, block_index * blk_rows, blk_rows, 1
            ).reshape(num_seqs, blk_rows, KV, DH)
            val_blk = lax.dynamic_slice_in_dim(
                value_piece, block_index * blk_rows, blk_rows, 1
            ).reshape(num_seqs, blk_rows, KV, DH)
            scores = (
                jnp.einsum(
                    "sqgrd,skgd->sgrqk", query_bf, key_blk, preferred_element_type=jnp.float32
                )
                * score_scale
            )
            causal = causal_at(kstart)
            scores = jnp.where(causal, scores, masked_value)
            new_top = jnp.maximum(row_max, jnp.max(scores, axis=-1))
            weights = jnp.where(causal, jnp.exp(scores - new_top[..., None]), 0.0)
            factor = jnp.exp(row_max - new_top)
            row_sum = row_sum * factor + jnp.sum(weights, axis=-1)
            weighted = weighted * factor[..., None] + jnp.einsum(
                "sgrqk,skgd->sgrqd",
                weights.astype(jnp.bfloat16),
                val_blk,
                preferred_element_type=jnp.float32,
            )
            return (new_top, row_sum, weighted)

        def skip_block(current):
            return current

        return lax.cond(kstart <= query_last, compute, skip_block, running)

    row_max, row_sum, weighted = lax.fori_loop(0, num_blocks, one_block, init_fwd)
    log_total = row_max + jnp.log(row_sum)
    attn_grouped = weighted / row_sum[..., None]
    attn_rows = attn_grouped.transpose(0, 3, 1, 2, 4).reshape(num_seqs, blk_rows, H * DH)
    attn_bf = attn_rows.astype(jnp.bfloat16)
    middle = input_rows + jnp.dot(attn_bf, out_full, preferred_element_type=jnp.float32)
    normed_two = norm_rows(middle, gain_second.astype(jnp.float32)).astype(jnp.bfloat16)
    gate_pre = jnp.dot(normed_two, gate_full, preferred_element_type=jnp.float32)
    up_pre = jnp.dot(normed_two, up_full, preferred_element_type=jnp.float32)
    hidden_bf = (jax.nn.silu(gate_pre) * up_pre).astype(jnp.bfloat16)
    output = middle + jnp.dot(hidden_bf, down_full, preferred_element_type=jnp.float32)
    back_params = (
        lax.all_gather(shards[0], ("dp", "ctx"), axis=0, tiled=True),
        lax.all_gather(shards[1], ("dp", "ctx"), axis=0, tiled=True),
        lax.all_gather(shards[2], ("dp", "ctx"), axis=0, tiled=True),
        lax.all_gather(shards[3], ("dp", "ctx"), axis=0, tiled=True),
        lax.all_gather(shards[4], ("dp", "ctx"), axis=0, tiled=True),
        lax.all_gather(shards[5], ("dp", "ctx"), axis=0, tiled=True),
        lax.all_gather(shards[6], ("dp", "ctx"), axis=0, tiled=True),
        lax.all_gather(shards[7], ("dp", "ctx"), axis=0, tiled=True),
        lax.all_gather(shards[8], ("dp", "ctx"), axis=0, tiled=True),
    )
    (
        back_first,
        back_second,
        query_back,
        key_back,
        value_back,
        out_back,
        gate_back,
        up_back,
        down_back,
    ) = back_params
    grad_top = d_out.astype(jnp.float32)
    grad_down_w = row_product(hidden_bf, d_out)
    grad_hidden = jnp.einsum("sbd,fd->sbf", d_out, down_back, preferred_element_type=jnp.float32)
    sigmoid_gate = jax.nn.sigmoid(gate_pre)
    grad_gate = (
        grad_hidden * up_pre * sigmoid_gate * (1.0 + gate_pre * (1.0 - sigmoid_gate))
    ).astype(jnp.bfloat16)
    grad_up = (grad_hidden * gate_pre * sigmoid_gate).astype(jnp.bfloat16)
    grad_gate_w = row_product(normed_two, grad_gate)
    grad_up_w = row_product(normed_two, grad_up)
    grad_normed_two = jnp.einsum(
        "sbf,df->sbd", grad_gate, gate_back, preferred_element_type=jnp.float32
    )
    grad_normed_two = grad_normed_two + jnp.einsum(
        "sbf,df->sbd", grad_up, up_back, preferred_element_type=jnp.float32
    )
    grad_mid_norm, gain_two_terms = norm_back(
        middle, back_second.astype(jnp.float32), grad_normed_two
    )
    grad_middle = grad_top + grad_mid_norm
    grad_mid_bf = grad_middle.astype(jnp.bfloat16)
    grad_out_w = row_product(attn_bf, grad_mid_bf)
    grad_attn_bf = jnp.einsum(
        "sbd,ed->sbe", grad_mid_bf, out_back, preferred_element_type=jnp.float32
    ).astype(jnp.bfloat16)
    grad_attn_grp = grad_attn_bf.reshape(num_seqs, blk_rows, KV, group_ratio, DH)
    row_delta = jnp.sum(
        grad_attn_grp.astype(jnp.float32)
        * attn_rows.reshape(num_seqs, blk_rows, KV, group_ratio, DH),
        axis=-1,
    ).transpose(0, 2, 3, 1)

    def block_terms(key_flat, value_flat, kstart):
        key_blk = key_flat.reshape(num_seqs, blk_rows, KV, DH)
        val_blk = value_flat.reshape(num_seqs, blk_rows, KV, DH)
        scores = (
            jnp.einsum("sqgrd,skgd->sgrqk", query_bf, key_blk, preferred_element_type=jnp.float32)
            * score_scale
        )
        causal = causal_at(kstart)
        probabilities = jnp.where(causal, jnp.exp(scores - log_total[..., None]), 0.0)
        grad_prob = jnp.einsum(
            "sqgrd,skgd->sgrqk", grad_attn_grp, val_blk, preferred_element_type=jnp.float32
        )
        grad_score = (probabilities * (grad_prob - row_delta[..., None])).astype(jnp.bfloat16)
        query_term = jnp.einsum(
            "sgrqk,skgd->sgrqd", grad_score, key_blk, preferred_element_type=jnp.float32
        )
        key_term = jnp.einsum(
            "sgrqk,sqgrd->skgd", grad_score, query_bf, preferred_element_type=jnp.float32
        ).reshape(num_seqs, blk_rows, KV * DH)
        val_term = jnp.einsum(
            "sgrqk,sqgrd->skgd",
            probabilities.astype(jnp.bfloat16),
            grad_attn_grp,
            preferred_element_type=jnp.float32,
        ).reshape(num_seqs, blk_rows, KV * DH)
        return (query_term, key_term, val_term)

    ctx_count = lax.axis_size("ctx")
    total_len = blk_rows * ctx_count
    init_back = (
        jnp.zeros(stat_shape + (DH,), jnp.float32),
        jnp.zeros((num_seqs, total_len, KV * DH), jnp.float32),
        jnp.zeros((num_seqs, total_len, KV * DH), jnp.float32),
    )
    attend_key_piece = lax.all_gather(key_bf, "ctx", axis=1, tiled=True)
    attend_value_piece = lax.all_gather(value_rows, "ctx", axis=1, tiled=True)
    num_blocks = attend_key_piece.shape[1] // blk_rows

    def one_block(block_index, running):
        kstart = block_index * blk_rows

        def compute(current):
            grad_query, grad_key, grad_value = current
            key_flat = lax.dynamic_slice_in_dim(
                attend_key_piece, block_index * blk_rows, blk_rows, 1
            )
            value_flat = lax.dynamic_slice_in_dim(
                attend_value_piece, block_index * blk_rows, blk_rows, 1
            )
            query_term, key_term, val_term = block_terms(key_flat, value_flat, kstart)
            grad_query = grad_query + query_term
            grad_key = lax.dynamic_update_slice_in_dim(
                grad_key,
                lax.dynamic_slice_in_dim(grad_key, kstart, blk_rows, 1) + key_term,
                kstart,
                1,
            )
            grad_value = lax.dynamic_update_slice_in_dim(
                grad_value,
                lax.dynamic_slice_in_dim(grad_value, kstart, blk_rows, 1) + val_term,
                kstart,
                1,
            )
            return (grad_query, grad_key, grad_value)

        def skip_block(current):
            return current

        return lax.cond(kstart <= query_last, compute, skip_block, running)

    grad_q_grp, grad_k_full, grad_v_full = lax.fori_loop(0, num_blocks, one_block, init_back)
    grad_k_loc, grad_v_loc = (
        lax.psum_scatter(
            (grad_k_full * score_scale).astype(jnp.bfloat16), "ctx", scatter_dimension=1, tiled=True
        ).astype(jnp.float32),
        lax.psum_scatter(
            grad_v_full.astype(jnp.bfloat16), "ctx", scatter_dimension=1, tiled=True
        ).astype(jnp.float32),
    )
    grad_q_rot = rounded(
        (grad_q_grp * score_scale).transpose(0, 3, 1, 2, 4).reshape(num_seqs, blk_rows, H, DH)
    )
    grad_k_rot = rounded(grad_k_loc).reshape(num_seqs, blk_rows, KV, DH)
    grad_v_bf = grad_v_loc.astype(jnp.bfloat16)
    grad_q_raw, query_gain_terms = norm_back(
        query_raw, query_scale, rotate_back(grad_q_rot, cosine, sine_part)
    )
    grad_k_raw, key_gain_terms = norm_back(
        key_raw, key_scale, rotate_back(grad_k_rot, cosine, sine_part)
    )
    grad_q_bf = grad_q_raw.reshape(num_seqs, blk_rows, H * DH).astype(jnp.bfloat16)
    grad_k_bf = grad_k_raw.reshape(num_seqs, blk_rows, KV * DH).astype(jnp.bfloat16)
    grad_query_w = row_product(normed_one, grad_q_bf)
    grad_key_w = row_product(normed_one, grad_k_bf)
    grad_value_w = row_product(normed_one, grad_v_bf)
    grad_normed_one = jnp.einsum(
        "sbe,de->sbd", grad_q_bf, query_back, preferred_element_type=jnp.float32
    )
    grad_normed_one = grad_normed_one + jnp.einsum(
        "sbe,de->sbd", grad_k_bf, key_back, preferred_element_type=jnp.float32
    )
    grad_normed_one = grad_normed_one + jnp.einsum(
        "sbe,de->sbd", grad_v_bf, value_back, preferred_element_type=jnp.float32
    )
    grad_in_norm, gain_one_terms = norm_back(
        input_rows, back_first.astype(jnp.float32), grad_normed_one
    )
    d_tokens = grad_middle + grad_in_norm
    head_sums = lax.psum((sum_rows(query_gain_terms), sum_rows(key_gain_terms)), ("dp", "ctx"))
    local_grads = (
        sum_rows(gain_one_terms),
        sum_rows(gain_two_terms),
        grad_query_w,
        grad_key_w,
        grad_value_w,
        grad_out_w,
        grad_gate_w,
        grad_up_w,
        grad_down_w,
    )
    reduced = (
        lax.psum_scatter(local_grads[0], ("dp", "ctx"), scatter_dimension=0, tiled=True),
        lax.psum_scatter(local_grads[1], ("dp", "ctx"), scatter_dimension=0, tiled=True),
        lax.psum_scatter(local_grads[2], ("dp", "ctx"), scatter_dimension=0, tiled=True),
        lax.psum_scatter(local_grads[3], ("dp", "ctx"), scatter_dimension=0, tiled=True),
        lax.psum_scatter(local_grads[4], ("dp", "ctx"), scatter_dimension=0, tiled=True),
        lax.psum_scatter(local_grads[5], ("dp", "ctx"), scatter_dimension=0, tiled=True),
        lax.psum_scatter(local_grads[6], ("dp", "ctx"), scatter_dimension=0, tiled=True),
        lax.psum_scatter(local_grads[7], ("dp", "ctx"), scatter_dimension=0, tiled=True),
        lax.psum_scatter(local_grads[8], ("dp", "ctx"), scatter_dimension=0, tiled=True),
    )
    return (
        output.astype(jnp.bfloat16),
        d_tokens,
        reduced[0],
        reduced[1],
        head_sums[0],
        head_sums[1],
        reduced[2],
        reduced[3],
        reduced[4],
        reduced[5],
        reduced[6],
        reduced[7],
        reduced[8],
    )


NT = (((1,), (1,)), ((), ()))
TN = (((0,), (0,)), ((), ()))
NN = (((1,), (0,)), ((), ()))


def dot(left, right, dims):
    return lax.dot_general(left, right, dims, preferred_element_type=jnp.float32)


def softmax_block(query_ref, key_ref, head, block, rows):
    end = (block + 1) * rows
    query_blk = query_ref[head, block * rows : end, :]
    scores = dot(query_blk, key_ref[0:end, :], NT) * (DH**-0.5)
    row = lax.broadcasted_iota(jnp.int32, scores.shape, 0) + block * rows
    col = lax.broadcasted_iota(jnp.int32, scores.shape, 1)
    scores = jnp.where(col <= row, scores, masked_value)
    shifted = jnp.exp(scores - jnp.max(scores, axis=-1, keepdims=True))
    total = jnp.sum(shifted, axis=-1, keepdims=True)
    return query_blk, shifted * (1.0 / total)


def attend_kernel(query_ref, key_ref, value_ref, out_ref, *, rows):
    heads, length = query_ref.shape[0], query_ref.shape[1]
    for block in range(length // rows):
        end = (block + 1) * rows
        for head in range(heads):
            _, probs = softmax_block(query_ref, key_ref, head, block, rows)
            mixed = dot(probs.astype(jnp.bfloat16), value_ref[0:end, :], NN)
            out_ref[block * rows : end, head * DH : (head + 1) * DH] = mixed.astype(jnp.bfloat16)


def attend_back_kernel(
    query_ref, key_ref, value_ref, grad_ref, dq_ref, dk_ref, dv_ref, dk_acc, dv_acc, *, rows
):
    heads, length = query_ref.shape[0], query_ref.shape[1]
    dk_acc[...] = jnp.zeros_like(dk_acc)
    dv_acc[...] = jnp.zeros_like(dv_acc)
    for block in range(length // rows):
        end = (block + 1) * rows
        for head in range(heads):
            query_blk, probs = softmax_block(query_ref, key_ref, head, block, rows)
            grad_blk = grad_ref[block * rows : end, head * DH : (head + 1) * DH]
            grad_probs = dot(grad_blk, value_ref[0:end, :], NT)
            delta = jnp.sum(probs * grad_probs, axis=-1, keepdims=True)
            grad_scores = (probs * (grad_probs - delta)).astype(jnp.bfloat16)
            dq = dot(grad_scores, key_ref[0:end, :], NN) * (DH**-0.5)
            dq_ref[head, block * rows : end, :] = dq.astype(jnp.bfloat16)
            dk_acc[0:end, :] += dot(grad_scores, query_blk, TN)
            dv_acc[0:end, :] += dot(probs.astype(jnp.bfloat16), grad_blk, TN)
    dk_ref[...] = (dk_acc[...] * (DH**-0.5)).astype(jnp.bfloat16)
    dv_ref[...] = dv_acc[...].astype(jnp.bfloat16)


def attend(query_rot, key_rot, value_rows, rows=256):
    heads, length, _ = query_rot.shape
    work = heads * length * length * DH
    return pl.pallas_call(
        lambda *refs: attend_kernel(*refs, rows=rows),
        out_shape=jax.ShapeDtypeStruct((length, heads * DH), jnp.bfloat16),
        in_specs=[pl.BlockSpec(memory_space=pltpu.VMEM)] * 3,
        out_specs=pl.BlockSpec(memory_space=pltpu.VMEM),
        cost_estimate=pl.CostEstimate(
            flops=4 * work, bytes_accessed=2 * length * DH * 6, transcendentals=work // DH
        ),
        name="attend",
    )(query_rot, key_rot, value_rows)


def attend_back(query_rot, key_rot, value_rows, grad_rows, rows=256):
    heads, length, _ = query_rot.shape
    work = heads * length * length * DH
    wide, thin = (heads, length, DH), (length, DH)
    return pl.pallas_call(
        lambda *refs: attend_back_kernel(*refs, rows=rows),
        out_shape=[jax.ShapeDtypeStruct(s, jnp.bfloat16) for s in (wide, thin, thin)],
        in_specs=[pl.BlockSpec(memory_space=pltpu.VMEM)] * 4,
        out_specs=[pl.BlockSpec(memory_space=pltpu.VMEM)] * 3,
        scratch_shapes=[pltpu.VMEM(thin, jnp.float32)] * 2,
        cost_estimate=pl.CostEstimate(
            flops=10 * work, bytes_accessed=2 * length * DH * 12, transcendentals=work // DH
        ),
        name="attend_back",
    )(query_rot, key_rot, value_rows, grad_rows)


AXES = ("y", "c", "z", "x")
SIZES = {"y": 2, "c": 2, "z": 4, "x": 2}


def swap(value, **flips):
    names = tuple(n for n in AXES if n in flips)
    mask, count = 0, 1
    for n in names:
        mask, count = mask * SIZES[n] + flips[n], count * SIZES[n]
    return lax.ppermute(value, names, [(i, i ^ mask) for i in range(count)])


def in_order(bit, own, other):
    return jnp.where(bit == 0, jnp.concatenate([own, other]), jnp.concatenate([other, own]))


def to_all(value, names):
    return lax.all_to_all(value, names, 0, 0, tiled=True)


def put(buffer, piece, starts):
    return lax.dynamic_update_slice(buffer, piece, starts)


def part(value, axis, index):
    return lax.dynamic_index_in_dim(value, index, axis, keepdims=False)


def gather_slots(rows):
    near = [rows] + [swap(rows, z=k) for k in (1, 2, 3)]
    far = [swap(r, c=1) for r in near]
    return jnp.concatenate(near + far)


def scatter_slots(partial):
    half = partial.shape[0] // 2
    rows = half // 4
    kept = partial[:half] + swap(partial[half:].astype(jnp.bfloat16), c=1).astype(jnp.float32)
    total = kept[:rows]
    for k in (1, 2, 3):
        piece = kept[k * rows : (k + 1) * rows].astype(jnp.bfloat16)
        total = total + swap(piece, z=k).astype(jnp.float32)
    return total


def split_device(
    tokens,
    positions,
    d_out,
    first_gain,
    second_gain,
    query_gain,
    key_gain,
    query_weight,
    key_weight,
    value_weight,
    out_weight,
    gate_weight,
    up_weight,
    down_weight,
):
    f32, bf16 = jnp.float32, jnp.bfloat16
    y, c, z, x = (lax.axis_index(n) for n in AXES)
    zero = jnp.zeros((), jnp.int32)
    block = z * 2 + x
    own = tokens[0]
    rows, width = own.shape
    blocks = 8
    length = rows * blocks
    thin = query_weight.shape[0]
    hidden = gate_weight.shape[1]
    piece = hidden // 8 // 2
    group = H // KV
    head_cols = group * DH

    small = jnp.concatenate(
        [first_gain.astype(f32), second_gain.astype(f32), positions[0].astype(f32)]
    ).reshape(1, -1)
    small = in_order(x, small, swap(small, x=1))
    small = in_order(z & 1, small, swap(small, z=1))
    small = in_order(z >> 1, small, swap(small, z=2))
    pos_seq = small[:, 2 * thin :].reshape(length)
    gains = small[:, : 2 * thin]
    gains = in_order(c, gains, swap(gains, c=1))
    gains = in_order(y, gains, swap(gains, y=1))
    gain_one = gains[:, :thin].reshape(1, width)
    gain_two = gains[:, thin:].reshape(1, width)

    near = [own] + [swap(own, z=k) for k in (1, 2, 3)]
    side = [swap(r, x=1) for r in near]
    seq_rows = jnp.zeros((blocks, rows, width), bf16)
    for k in range(4):
        for j, source in ((0, near), (1, side)):
            seq_rows = put(seq_rows, source[k][None], (block ^ (2 * k + j), zero, zero))
    seq_rows = seq_rows.reshape(length, width)

    qkv_rows = jnp.concatenate(
        [
            query_weight.reshape(thin, KV, head_cols),
            key_weight.reshape(thin, KV, DH),
            value_weight.reshape(thin, KV, DH),
        ],
        axis=2,
    )
    qkv_cols = to_all(qkv_rows.transpose(1, 0, 2), ("z", "x")).reshape(1, length // 4, -1)
    qkv_cols = in_order(c, qkv_cols, swap(qkv_cols, c=1))
    qkv_cols = in_order(y, qkv_cols, swap(qkv_cols, y=1)).reshape(width, -1)

    def by_owner(weight):
        return weight.reshape(thin, 2, 2, 4, piece).transpose(2, 3, 0, 1, 4).reshape(8, 1, thin, 2 * piece)

    gate_up = to_all(jnp.concatenate([by_owner(gate_weight), by_owner(up_weight)], axis=1), ("c", "z"))
    hid = 2 * piece
    wide_parts = {(0, 0): gate_up}
    down_parts = {(0, 0): down_weight}
    for i, j in ((0, 1), (1, 0), (1, 1)):
        flips = {n: 1 for n, on in (("y", i), ("x", j)) if on}
        wide_parts[i, j] = swap(gate_up, **flips)
        down_parts[i, j] = swap(down_weight, **flips)
    gate_buf = jnp.zeros((2, 8, 2, thin, hid), bf16)
    up_buf = jnp.zeros((2, 8, 2, thin, hid), bf16)
    down_buf = jnp.zeros((2, 2, piece // 2, width), bf16)
    for (i, j), got in wide_parts.items():
        at = (y ^ i, zero, x ^ j, zero, zero)
        gate_buf = put(gate_buf, got[:, 0][None, :, None], at)
        up_buf = put(up_buf, got[:, 1][None, :, None], at)
        down_buf = put(down_buf, down_parts[i, j][None, None], (y ^ i, x ^ j, zero, zero))
    gate_full = gate_buf.reshape(width, hid)
    up_full = up_buf.reshape(width, hid)
    down_full = down_buf.reshape(hid, width)

    def all_rows(weight):
        stacked = jnp.zeros((4,) + weight.shape, bf16)
        stacked = put(stacked, weight[None], (z, zero, zero))
        for k in (1, 2, 3):
            stacked = put(stacked, swap(weight, z=k)[None], (z ^ k, zero, zero))
        stacked = stacked[:, None]
        other = swap(stacked, x=1)
        stacked = jnp.where(
            x == 0, jnp.concatenate([stacked, other], 1), jnp.concatenate([other, stacked], 1)
        ).reshape((1, 8) + weight.shape)
        stacked = in_order(c, stacked, swap(stacked, c=1))
        stacked = in_order(y, stacked, swap(stacked, y=1))
        return stacked.reshape(-1, weight.shape[1])

    out_full = all_rows(out_weight)
    qkv_full = all_rows(qkv_rows.reshape(thin, -1))

    grad_slots = gather_slots(d_out[0])

    query_scale, key_scale = query_gain.astype(f32), key_gain.astype(f32)
    cosine, sine_part = rope_tables(pos_seq)
    normed_seq = norm_rows(seq_rows.astype(f32), gain_one).astype(bf16)
    raw = dot(normed_seq, qkv_cols, NN)
    query_raw = raw[:, :head_cols].reshape(length, group, DH)
    key_raw = raw[:, head_cols : head_cols + DH].reshape(length, 1, DH)
    value_bf = raw[:, head_cols + DH :].astype(bf16)
    query_bf = rotate(norm_rows(query_raw, query_scale), cosine, sine_part).astype(bf16)
    query_bf = query_bf.transpose(1, 0, 2)
    key_bf = rotate(norm_rows(key_raw, key_scale), cosine, sine_part).astype(bf16)[:, 0]
    mixed = attend(query_bf, key_bf, value_bf)
    mixed = to_all(mixed.reshape(blocks, rows, head_cols), ("z", "x"))
    attn_bf = mixed.transpose(1, 0, 2).reshape(rows, H * DH)

    input_rows = own.astype(f32)
    middle = input_rows + dot(attn_bf, out_full, NN)
    normed_two = norm_rows(middle, gain_two).astype(bf16)
    slots = gather_slots(normed_two)
    gate_pre = dot(slots, gate_full, NN)
    up_pre = dot(slots, up_full, NN)
    sigmoid_gate = jax.nn.sigmoid(gate_pre)
    hidden_bf = (gate_pre * sigmoid_gate * up_pre).astype(bf16)
    grad_hidden = dot(grad_slots, down_full, NT)
    grad_gate = (
        grad_hidden * up_pre * sigmoid_gate * (1.0 + gate_pre * (1.0 - sigmoid_gate))
    ).astype(bf16)
    grad_up = (grad_hidden * gate_pre * sigmoid_gate).astype(bf16)
    grad_normed_two = scatter_slots(dot(grad_gate, gate_full, NT) + dot(grad_up, up_full, NT))
    grad_mid_norm, _ = norm_back(middle, gain_two, grad_normed_two)
    grad_middle = d_out[0].astype(f32) + grad_mid_norm
    grad_mid_bf = grad_middle.astype(bf16)
    grad_attn = dot(grad_mid_bf, out_full, NT).astype(bf16)
    grad_attn = to_all(grad_attn.reshape(rows, KV, head_cols).transpose(1, 0, 2), ("z", "x"))

    output = middle + scatter_slots(dot(hidden_bf, down_full, NN))

    grad_down_w = dot(hidden_bf, grad_slots, TN).reshape(2, 2, piece // 2, width)
    grad_gate_w = dot(slots, grad_gate, TN).reshape(2, 8, 2, thin, hid)
    grad_up_w = dot(slots, grad_up, TN).reshape(2, 8, 2, thin, hid)

    def square_sum(value, y_axis, x_axis):
        def of(i, j):
            return part(part(value, x_axis, x ^ j), y_axis, y ^ i)

        total = of(0, 0)
        for i, j in ((0, 1), (1, 0), (1, 1)):
            flips = {n: 1 for n, on in (("y", i), ("x", j)) if on}
            total = total + swap(of(i, j).astype(bf16), **flips).astype(f32)
        return total

    grad_down_w = square_sum(grad_down_w, 0, 1)
    grad_wide = jnp.stack([square_sum(grad_gate_w, 0, 2), square_sum(grad_up_w, 0, 2)], axis=1)
    grad_wide = to_all(grad_wide, ("c", "z"))

    def from_owner(value):
        value = value.reshape(2, 4, thin, 2, piece).transpose(2, 3, 0, 1, 4)
        return value.reshape(thin, hidden)

    grad_gate_w = from_owner(grad_wide[:, 0])
    grad_up_w = from_owner(grad_wide[:, 1])
    second_gain_grad = jnp.sum(
        gate_weight.astype(f32) * grad_gate_w + up_weight.astype(f32) * grad_up_w, axis=1
    ) / second_gain.astype(f32)

    grad_out_w = dot(attn_bf, grad_mid_bf, TN).reshape(2, 2, 4, 2, thin, width)

    def halve(value, axis, at, **flips):
        sent = part(value, axis, 1 - at).astype(bf16)
        return part(value, axis, at) + swap(sent, **flips).astype(f32)

    grad_out_w = halve(grad_out_w, 1, c, c=1)
    grad_out_w = halve(grad_out_w, 0, y, y=1)
    grad_out_w = halve(grad_out_w, 1, x, x=1)
    total = part(grad_out_w, 0, z)
    for k in (1, 2, 3):
        total = total + swap(part(grad_out_w, 0, z ^ k).astype(bf16), z=k).astype(f32)
    grad_out_w = total

    dq, dk, dv = attend_back(query_bf, key_bf, value_bf, grad_attn.reshape(length, head_cols))
    dq = dq.transpose(1, 0, 2).astype(f32)
    dk = dk[:, None].astype(f32)
    dq, query_terms = norm_back(query_raw, query_scale, rotate_back(dq, cosine, sine_part))
    dk, key_terms = norm_back(key_raw, key_scale, rotate_back(dk, cosine, sine_part))
    head_sums = jnp.stack([sum_rows(query_terms), sum_rows(key_terms)])
    for flips in ({"c": 1}, {"x": 1}, {"z": 1}, {"z": 2}, {"y": 1}):
        head_sums = head_sums + swap(head_sums, **flips)
    grad_qkv = jnp.concatenate(
        [
            dq.reshape(length, head_cols).astype(bf16),
            dk.reshape(length, DH).astype(bf16),
            dv,
        ],
        axis=1,
    )
    grad_own = to_all(grad_qkv.reshape(blocks, rows, -1), ("z", "x")).transpose(1, 0, 2)
    grad_normed_one = dot(grad_own.reshape(rows, -1), qkv_full, NT)
    grad_in_norm, _ = norm_back(input_rows, gain_one, grad_normed_one)
    d_tokens = grad_middle + grad_in_norm

    grad_qkv_w = dot(normed_seq, grad_qkv, TN).reshape(2, 2, width // 4, -1)
    sent = part(grad_qkv_w, 1, 1 - c)
    grad_qkv_w = part(grad_qkv_w, 1, c) + swap(sent, c=1)
    sent = part(grad_qkv_w, 0, 1 - y)
    grad_qkv_w = part(grad_qkv_w, 0, y) + swap(sent, y=1)
    grad_qkv_w = to_all(grad_qkv_w.reshape(blocks, thin, -1), ("z", "x")).transpose(1, 0, 2)
    grad_query_w = grad_qkv_w[:, :, :head_cols].reshape(thin, -1)
    grad_key_w = grad_qkv_w[:, :, head_cols : head_cols + DH].reshape(thin, -1)
    grad_value_w = grad_qkv_w[:, :, head_cols + DH :].reshape(thin, -1)
    first_gain_grad = jnp.sum(qkv_rows.astype(f32) * grad_qkv_w, axis=(1, 2)) / first_gain.astype(f32)
    return (
        output.astype(bf16)[None],
        d_tokens[None],
        first_gain_grad,
        second_gain_grad,
        head_sums[0],
        head_sums[1],
        grad_query_w,
        grad_key_w,
        grad_value_w,
        grad_out_w,
        grad_gate_w,
        grad_up_w,
        grad_down_w,
    )


def split_solution(mesh):
    inner = Mesh(mesh.devices.reshape([SIZES[n] for n in AXES]), AXES)
    every, dp, ctx = AXES, ("y", "c"), ("z", "x")
    seq, vec, mat = P(dp, ctx, None), P(every), P(every, None)
    return jax.shard_map(
        split_device,
        mesh=inner,
        in_specs=(seq, P(dp, ctx), seq, vec, vec, P(), P()) + (mat,) * 7,
        out_specs=(seq, seq, vec, vec, P(), P()) + (mat,) * 7,
        check_vma=False,
    )


def solution(mesh):
    if mesh.shape["dp"] == 4 and mesh.shape["ctx"] == KV:
        return split_solution(mesh)
    in_specs = (
        P("dp", "ctx", None),
        P("dp", "ctx"),
        P("dp", "ctx", None),
        P(("dp", "ctx")),
        P(("dp", "ctx")),
        P(),
        P(),
        P(("dp", "ctx"), None),
        P(("dp", "ctx"), None),
        P(("dp", "ctx"), None),
        P(("dp", "ctx"), None),
        P(("dp", "ctx"), None),
        P(("dp", "ctx"), None),
        P(("dp", "ctx"), None),
    )
    out_specs = (
        P("dp", "ctx", None),
        P("dp", "ctx", None),
        P(("dp", "ctx")),
        P(("dp", "ctx")),
        P(),
        P(),
        P(("dp", "ctx"), None),
        P(("dp", "ctx"), None),
        P(("dp", "ctx"), None),
        P(("dp", "ctx"), None),
        P(("dp", "ctx"), None),
        P(("dp", "ctx"), None),
        P(("dp", "ctx"), None),
    )
    return jax.shard_map(
        generic_device, mesh=mesh, in_specs=in_specs, out_specs=out_specs, check_vma=False
    )
```

```python
import jax
import jax.numpy as jnp
from jax import lax
from jax.experimental import pallas as pl
from jax.experimental.pallas import tpu as pltpu
from jax.sharding import Mesh, PartitionSpec as P

H = 16
KV = 8
DH = 64


epsilon = 1e-05
rope_base = 1000000.0
masked_value = -1e30


def norm_rows(values, gain_row):
    return (
        values * lax.rsqrt(jnp.mean(values * values, axis=-1, keepdims=True) + epsilon) * gain_row
    )


def norm_back(values, gain_row, grad_out):
    scale_rows = lax.rsqrt(jnp.mean(values * values, axis=-1, keepdims=True) + epsilon)
    normed = values * scale_rows
    grad_normed = grad_out * gain_row
    grad_in = scale_rows * (
        grad_normed - normed * jnp.mean(grad_normed * normed, axis=-1, keepdims=True)
    )
    return (grad_in, grad_out * normed)


def rope_tables(seq_positions):
    frequency = rope_base ** (-jnp.arange(0, DH, 2, dtype=jnp.float32) / DH)
    angles = seq_positions.astype(jnp.float32)[..., None] * frequency
    return (jnp.cos(angles)[..., None, :], jnp.sin(angles)[..., None, :])


def rotate(values, cosine, sine_part):
    half_size = values.shape[-1] // 2
    half_one = values[..., :half_size]
    half_two = values[..., half_size:]
    return jnp.concatenate(
        [half_one * cosine - half_two * sine_part, half_two * cosine + half_one * sine_part],
        axis=-1,
    )


def rotate_back(grads_in, cosine, sine_part):
    half_size = grads_in.shape[-1] // 2
    half_one = grads_in[..., :half_size]
    half_two = grads_in[..., half_size:]
    return jnp.concatenate(
        [half_one * cosine + half_two * sine_part, half_two * cosine - half_one * sine_part],
        axis=-1,
    )


def sum_rows(values):
    return jnp.sum(values.reshape(-1, values.shape[-1]), axis=0)


def row_product(left_rows, right_rows):
    return jnp.einsum("sba,sbc->ac", left_rows, right_rows, preferred_element_type=jnp.float32)


def rounded(values):
    return lax.optimization_barrier(values.astype(jnp.bfloat16)).astype(jnp.float32)


def generic_device(
    tokens,
    positions,
    d_out,
    first_gain,
    second_gain,
    query_gain,
    key_gain,
    query_weight,
    key_weight,
    value_weight,
    out_weight,
    gate_weight,
    up_weight,
    down_weight,
):
    num_seqs, blk_rows = (tokens.shape[0], tokens.shape[1])
    group_ratio = H // KV
    score_scale = DH ** (-0.5)
    shards = (
        first_gain,
        second_gain,
        query_weight,
        key_weight,
        value_weight,
        out_weight,
        gate_weight,
        up_weight,
        down_weight,
    )
    full_params = (
        lax.all_gather(shards[0], ("dp", "ctx"), axis=0, tiled=True),
        lax.all_gather(shards[1], ("dp", "ctx"), axis=0, tiled=True),
        lax.all_gather(shards[2], ("dp", "ctx"), axis=0, tiled=True),
        lax.all_gather(shards[3], ("dp", "ctx"), axis=0, tiled=True),
        lax.all_gather(shards[4], ("dp", "ctx"), axis=0, tiled=True),
        lax.all_gather(shards[5], ("dp", "ctx"), axis=0, tiled=True),
        lax.all_gather(shards[6], ("dp", "ctx"), axis=0, tiled=True),
        lax.all_gather(shards[7], ("dp", "ctx"), axis=0, tiled=True),
        lax.all_gather(shards[8], ("dp", "ctx"), axis=0, tiled=True),
    )
    (
        gain_first,
        gain_second,
        query_full,
        key_full,
        value_full,
        out_full,
        gate_full,
        up_full,
        down_full,
    ) = full_params
    query_scale = query_gain.astype(jnp.float32)
    key_scale = key_gain.astype(jnp.float32)
    input_rows = tokens.astype(jnp.float32)
    cosine, sine_part = rope_tables(positions)
    normed_one = norm_rows(input_rows, gain_first.astype(jnp.float32)).astype(jnp.bfloat16)
    query_raw = jnp.dot(normed_one, query_full, preferred_element_type=jnp.float32).reshape(
        num_seqs, blk_rows, H, DH
    )
    key_raw = jnp.dot(normed_one, key_full, preferred_element_type=jnp.float32).reshape(
        num_seqs, blk_rows, KV, DH
    )
    value_rows = jnp.dot(normed_one, value_full, preferred_element_type=jnp.float32).astype(
        jnp.bfloat16
    )
    query_rot = rotate(norm_rows(query_raw, query_scale), cosine, sine_part)
    key_rot = rotate(norm_rows(key_raw, key_scale), cosine, sine_part)
    query_bf = query_rot.astype(jnp.bfloat16).reshape(num_seqs, blk_rows, KV, group_ratio, DH)
    key_bf = key_rot.astype(jnp.bfloat16).reshape(num_seqs, blk_rows, KV * DH)
    own_index = lax.axis_index("ctx")
    query_base = own_index * blk_rows
    row_ids = jnp.arange(blk_rows, dtype=jnp.int32)
    query_pos = query_base + row_ids
    query_last = query_base + blk_rows - 1

    def causal_at(key_first):
        return (key_first + row_ids)[None, :] <= query_pos[:, None]

    stat_shape = (num_seqs, KV, group_ratio, blk_rows)
    init_fwd = (
        jnp.full(stat_shape, masked_value, jnp.float32),
        jnp.zeros(stat_shape, jnp.float32),
        jnp.zeros(stat_shape + (DH,), jnp.float32),
    )
    key_piece = lax.all_gather(key_bf, "ctx", axis=1, tiled=True)
    value_piece = lax.all_gather(value_rows, "ctx", axis=1, tiled=True)
    num_blocks = key_piece.shape[1] // blk_rows

    def one_block(block_index, running):
        kstart = block_index * blk_rows

        def compute(current):
            row_max, row_sum, weighted = current
            key_blk = lax.dynamic_slice_in_dim(
                key_piece, block_index * blk_rows, blk_rows, 1
            ).reshape(num_seqs, blk_rows, KV, DH)
            val_blk = lax.dynamic_slice_in_dim(
                value_piece, block_index * blk_rows, blk_rows, 1
            ).reshape(num_seqs, blk_rows, KV, DH)
            scores = (
                jnp.einsum(
                    "sqgrd,skgd->sgrqk", query_bf, key_blk, preferred_element_type=jnp.float32
                )
                * score_scale
            )
            causal = causal_at(kstart)
            scores = jnp.where(causal, scores, masked_value)
            new_top = jnp.maximum(row_max, jnp.max(scores, axis=-1))
            weights = jnp.where(causal, jnp.exp(scores - new_top[..., None]), 0.0)
            factor = jnp.exp(row_max - new_top)
            row_sum = row_sum * factor + jnp.sum(weights, axis=-1)
            weighted = weighted * factor[..., None] + jnp.einsum(
                "sgrqk,skgd->sgrqd",
                weights.astype(jnp.bfloat16),
                val_blk,
                preferred_element_type=jnp.float32,
            )
            return (new_top, row_sum, weighted)

        def skip_block(current):
            return current

        return lax.cond(kstart <= query_last, compute, skip_block, running)

    row_max, row_sum, weighted = lax.fori_loop(0, num_blocks, one_block, init_fwd)
    log_total = row_max + jnp.log(row_sum)
    attn_grouped = weighted / row_sum[..., None]
    attn_rows = attn_grouped.transpose(0, 3, 1, 2, 4).reshape(num_seqs, blk_rows, H * DH)
    attn_bf = attn_rows.astype(jnp.bfloat16)
    middle = input_rows + jnp.dot(attn_bf, out_full, preferred_element_type=jnp.float32)
    normed_two = norm_rows(middle, gain_second.astype(jnp.float32)).astype(jnp.bfloat16)
    gate_pre = jnp.dot(normed_two, gate_full, preferred_element_type=jnp.float32)
    up_pre = jnp.dot(normed_two, up_full, preferred_element_type=jnp.float32)
    hidden_bf = (jax.nn.silu(gate_pre) * up_pre).astype(jnp.bfloat16)
    output = middle + jnp.dot(hidden_bf, down_full, preferred_element_type=jnp.float32)
    back_params = (
        lax.all_gather(shards[0], ("dp", "ctx"), axis=0, tiled=True),
        lax.all_gather(shards[1], ("dp", "ctx"), axis=0, tiled=True),
        lax.all_gather(shards[2], ("dp", "ctx"), axis=0, tiled=True),
        lax.all_gather(shards[3], ("dp", "ctx"), axis=0, tiled=True),
        lax.all_gather(shards[4], ("dp", "ctx"), axis=0, tiled=True),
        lax.all_gather(shards[5], ("dp", "ctx"), axis=0, tiled=True),
        lax.all_gather(shards[6], ("dp", "ctx"), axis=0, tiled=True),
        lax.all_gather(shards[7], ("dp", "ctx"), axis=0, tiled=True),
        lax.all_gather(shards[8], ("dp", "ctx"), axis=0, tiled=True),
    )
    (
        back_first,
        back_second,
        query_back,
        key_back,
        value_back,
        out_back,
        gate_back,
        up_back,
        down_back,
    ) = back_params
    grad_top = d_out.astype(jnp.float32)
    grad_down_w = row_product(hidden_bf, d_out)
    grad_hidden = jnp.einsum("sbd,fd->sbf", d_out, down_back, preferred_element_type=jnp.float32)
    sigmoid_gate = jax.nn.sigmoid(gate_pre)
    grad_gate = (
        grad_hidden * up_pre * sigmoid_gate * (1.0 + gate_pre * (1.0 - sigmoid_gate))
    ).astype(jnp.bfloat16)
    grad_up = (grad_hidden * gate_pre * sigmoid_gate).astype(jnp.bfloat16)
    grad_gate_w = row_product(normed_two, grad_gate)
    grad_up_w = row_product(normed_two, grad_up)
    grad_normed_two = jnp.einsum(
        "sbf,df->sbd", grad_gate, gate_back, preferred_element_type=jnp.float32
    )
    grad_normed_two = grad_normed_two + jnp.einsum(
        "sbf,df->sbd", grad_up, up_back, preferred_element_type=jnp.float32
    )
    grad_mid_norm, gain_two_terms = norm_back(
        middle, back_second.astype(jnp.float32), grad_normed_two
    )
    grad_middle = grad_top + grad_mid_norm
    grad_mid_bf = grad_middle.astype(jnp.bfloat16)
    grad_out_w = row_product(attn_bf, grad_mid_bf)
    grad_attn_bf = jnp.einsum(
        "sbd,ed->sbe", grad_mid_bf, out_back, preferred_element_type=jnp.float32
    ).astype(jnp.bfloat16)
    grad_attn_grp = grad_attn_bf.reshape(num_seqs, blk_rows, KV, group_ratio, DH)
    row_delta = jnp.sum(
        grad_attn_grp.astype(jnp.float32)
        * attn_rows.reshape(num_seqs, blk_rows, KV, group_ratio, DH),
        axis=-1,
    ).transpose(0, 2, 3, 1)

    def block_terms(key_flat, value_flat, kstart):
        key_blk = key_flat.reshape(num_seqs, blk_rows, KV, DH)
        val_blk = value_flat.reshape(num_seqs, blk_rows, KV, DH)
        scores = (
            jnp.einsum("sqgrd,skgd->sgrqk", query_bf, key_blk, preferred_element_type=jnp.float32)
            * score_scale
        )
        causal = causal_at(kstart)
        probabilities = jnp.where(causal, jnp.exp(scores - log_total[..., None]), 0.0)
        grad_prob = jnp.einsum(
            "sqgrd,skgd->sgrqk", grad_attn_grp, val_blk, preferred_element_type=jnp.float32
        )
        grad_score = (probabilities * (grad_prob - row_delta[..., None])).astype(jnp.bfloat16)
        query_term = jnp.einsum(
            "sgrqk,skgd->sgrqd", grad_score, key_blk, preferred_element_type=jnp.float32
        )
        key_term = jnp.einsum(
            "sgrqk,sqgrd->skgd", grad_score, query_bf, preferred_element_type=jnp.float32
        ).reshape(num_seqs, blk_rows, KV * DH)
        val_term = jnp.einsum(
            "sgrqk,sqgrd->skgd",
            probabilities.astype(jnp.bfloat16),
            grad_attn_grp,
            preferred_element_type=jnp.float32,
        ).reshape(num_seqs, blk_rows, KV * DH)
        return (query_term, key_term, val_term)

    ctx_count = lax.axis_size("ctx")
    total_len = blk_rows * ctx_count
    init_back = (
        jnp.zeros(stat_shape + (DH,), jnp.float32),
        jnp.zeros((num_seqs, total_len, KV * DH), jnp.float32),
        jnp.zeros((num_seqs, total_len, KV * DH), jnp.float32),
    )
    attend_key_piece = lax.all_gather(key_bf, "ctx", axis=1, tiled=True)
    attend_value_piece = lax.all_gather(value_rows, "ctx", axis=1, tiled=True)
    num_blocks = attend_key_piece.shape[1] // blk_rows

    def one_block(block_index, running):
        kstart = block_index * blk_rows

        def compute(current):
            grad_query, grad_key, grad_value = current
            key_flat = lax.dynamic_slice_in_dim(
                attend_key_piece, block_index * blk_rows, blk_rows, 1
            )
            value_flat = lax.dynamic_slice_in_dim(
                attend_value_piece, block_index * blk_rows, blk_rows, 1
            )
            query_term, key_term, val_term = block_terms(key_flat, value_flat, kstart)
            grad_query = grad_query + query_term
            grad_key = lax.dynamic_update_slice_in_dim(
                grad_key,
                lax.dynamic_slice_in_dim(grad_key, kstart, blk_rows, 1) + key_term,
                kstart,
                1,
            )
            grad_value = lax.dynamic_update_slice_in_dim(
                grad_value,
                lax.dynamic_slice_in_dim(grad_value, kstart, blk_rows, 1) + val_term,
                kstart,
                1,
            )
            return (grad_query, grad_key, grad_value)

        def skip_block(current):
            return current

        return lax.cond(kstart <= query_last, compute, skip_block, running)

    grad_q_grp, grad_k_full, grad_v_full = lax.fori_loop(0, num_blocks, one_block, init_back)
    grad_k_loc, grad_v_loc = (
        lax.psum_scatter(
            (grad_k_full * score_scale).astype(jnp.bfloat16), "ctx", scatter_dimension=1, tiled=True
        ).astype(jnp.float32),
        lax.psum_scatter(
            grad_v_full.astype(jnp.bfloat16), "ctx", scatter_dimension=1, tiled=True
        ).astype(jnp.float32),
    )
    grad_q_rot = rounded(
        (grad_q_grp * score_scale).transpose(0, 3, 1, 2, 4).reshape(num_seqs, blk_rows, H, DH)
    )
    grad_k_rot = rounded(grad_k_loc).reshape(num_seqs, blk_rows, KV, DH)
    grad_v_bf = grad_v_loc.astype(jnp.bfloat16)
    grad_q_raw, query_gain_terms = norm_back(
        query_raw, query_scale, rotate_back(grad_q_rot, cosine, sine_part)
    )
    grad_k_raw, key_gain_terms = norm_back(
        key_raw, key_scale, rotate_back(grad_k_rot, cosine, sine_part)
    )
    grad_q_bf = grad_q_raw.reshape(num_seqs, blk_rows, H * DH).astype(jnp.bfloat16)
    grad_k_bf = grad_k_raw.reshape(num_seqs, blk_rows, KV * DH).astype(jnp.bfloat16)
    grad_query_w = row_product(normed_one, grad_q_bf)
    grad_key_w = row_product(normed_one, grad_k_bf)
    grad_value_w = row_product(normed_one, grad_v_bf)
    grad_normed_one = jnp.einsum(
        "sbe,de->sbd", grad_q_bf, query_back, preferred_element_type=jnp.float32
    )
    grad_normed_one = grad_normed_one + jnp.einsum(
        "sbe,de->sbd", grad_k_bf, key_back, preferred_element_type=jnp.float32
    )
    grad_normed_one = grad_normed_one + jnp.einsum(
        "sbe,de->sbd", grad_v_bf, value_back, preferred_element_type=jnp.float32
    )
    grad_in_norm, gain_one_terms = norm_back(
        input_rows, back_first.astype(jnp.float32), grad_normed_one
    )
    d_tokens = grad_middle + grad_in_norm
    head_sums = lax.psum((sum_rows(query_gain_terms), sum_rows(key_gain_terms)), ("dp", "ctx"))
    local_grads = (
        sum_rows(gain_one_terms),
        sum_rows(gain_two_terms),
        grad_query_w,
        grad_key_w,
        grad_value_w,
        grad_out_w,
        grad_gate_w,
        grad_up_w,
        grad_down_w,
    )
    reduced = (
        lax.psum_scatter(local_grads[0], ("dp", "ctx"), scatter_dimension=0, tiled=True),
        lax.psum_scatter(local_grads[1], ("dp", "ctx"), scatter_dimension=0, tiled=True),
        lax.psum_scatter(local_grads[2], ("dp", "ctx"), scatter_dimension=0, tiled=True),
        lax.psum_scatter(local_grads[3], ("dp", "ctx"), scatter_dimension=0, tiled=True),
        lax.psum_scatter(local_grads[4], ("dp", "ctx"), scatter_dimension=0, tiled=True),
        lax.psum_scatter(local_grads[5], ("dp", "ctx"), scatter_dimension=0, tiled=True),
        lax.psum_scatter(local_grads[6], ("dp", "ctx"), scatter_dimension=0, tiled=True),
        lax.psum_scatter(local_grads[7], ("dp", "ctx"), scatter_dimension=0, tiled=True),
        lax.psum_scatter(local_grads[8], ("dp", "ctx"), scatter_dimension=0, tiled=True),
    )
    return (
        output.astype(jnp.bfloat16),
        d_tokens,
        reduced[0],
        reduced[1],
        head_sums[0],
        head_sums[1],
        reduced[2],
        reduced[3],
        reduced[4],
        reduced[5],
        reduced[6],
        reduced[7],
        reduced[8],
    )


NT = (((1,), (1,)), ((), ()))
TN = (((0,), (0,)), ((), ()))
NN = (((1,), (0,)), ((), ()))
AXES = ("y", "c", "z", "x")
SIZES = {"y": 2, "c": 2, "z": 4, "x": 2}
f32, bf16 = jnp.float32, jnp.bfloat16


def dot(left, right, dims):
    return lax.dot_general(left, right, dims, preferred_element_type=f32)


def kernel_call(body, outs, *args, scratch=(), flops=0, transcendentals=0, name, scalars=None):
    vmem = pl.BlockSpec(memory_space=pltpu.VMEM)
    in_specs = [vmem] * len(args)
    if scalars is not None:
        in_specs = [pl.BlockSpec(memory_space=pltpu.SMEM)] + in_specs
        args = (scalars,) + args
    moved = sum(a.size * a.dtype.itemsize for a in args)
    moved += sum(o.size * o.dtype.itemsize for o in outs)
    return pl.pallas_call(
        body,
        out_shape=list(outs),
        in_specs=in_specs,
        out_specs=[vmem] * len(outs),
        scratch_shapes=list(scratch),
        cost_estimate=pl.CostEstimate(
            flops=flops, bytes_accessed=moved, transcendentals=transcendentals
        ),
        name=name,
    )(*args)


def shape(dims, dtype):
    return jax.ShapeDtypeStruct(dims, dtype)


def aligned(index, size):
    return pl.ds(pl.multiple_of(index * size, size), size)


def swap(value, **flips):
    names = tuple(n for n in AXES if n in flips)
    mask, count = 0, 1
    for n in names:
        mask, count = mask * SIZES[n] + flips[n], count * SIZES[n]
    return lax.ppermute(value, names, [(i, i ^ mask) for i in range(count)])


def to_all(value, names):
    return lax.all_to_all(value, names, 0, 0, tiled=True)


def after(value, *others):
    return lax.optimization_barrier((value,) + others)[0]


def part(value, axis, index):
    return lax.dynamic_index_in_dim(value, index, axis, keepdims=False)


def cut_kernel(gate_ref, up_ref, query_ref, key_ref, value_ref, extra_ref, wide_ref, cols_ref, rows_ref):
    thin = gate_ref.shape[0]
    piece = gate_ref.shape[1] // 16
    for which, ref in ((0, gate_ref), (1, up_ref)):
        for y in range(2):
            for owner in range(8):
                start = (y * 8 + owner) * piece
                wide_ref[owner, which, :, y * piece : (y + 1) * piece] = ref[:, start : start + piece]
    for t in range(KV):
        cols_ref[t, 0:thin, 0:128] = query_ref[:, t * 128 : (t + 1) * 128]
        cols_ref[t, 0:thin, 128:192] = key_ref[:, t * DH : (t + 1) * DH]
        cols_ref[t, 0:thin, 192:256] = value_ref[:, t * DH : (t + 1) * DH]
        cols_ref[t, thin : thin + 16, :] = extra_ref[...]
        rows_ref[:, t * 256 : t * 256 + 128] = query_ref[:, t * 128 : (t + 1) * 128]
        rows_ref[:, t * 256 + 128 : t * 256 + 192] = key_ref[:, t * DH : (t + 1) * DH]
        rows_ref[:, t * 256 + 192 : t * 256 + 256] = value_ref[:, t * DH : (t + 1) * DH]


def low_lanes(dims):
    return lax.broadcasted_iota(jnp.int32, dims, 1) < DH


def halves_swapped(values):
    first = lax.broadcasted_iota(jnp.int32, values.shape, 1) % DH < DH // 2
    return jnp.where(first, pltpu.roll(values, 128 - DH // 2, 1), pltpu.roll(values, DH // 2, 1))


def head_means(values):
    low = low_lanes(values.shape)
    first = jnp.sum(jnp.where(low, values, 0.0), axis=-1, keepdims=True)
    second = jnp.sum(jnp.where(low, 0.0, values), axis=-1, keepdims=True)
    return jnp.where(low, first, second) * (1.0 / DH)


def head_scale(values):
    return lax.rsqrt(head_means(values * values) + epsilon)


def softmax_block(query_blk, key_ref, block, rows):
    end = (block + 1) * rows
    scores = dot(query_blk, key_ref[0:end, :], NT) * (DH**-0.5)
    row = lax.broadcasted_iota(jnp.int32, scores.shape, 0) + block * rows
    col = lax.broadcasted_iota(jnp.int32, scores.shape, 1)
    scores = jnp.where(col <= row, scores, masked_value)
    shifted = jnp.exp(scores - jnp.max(scores, axis=-1, keepdims=True))
    total = jnp.sum(shifted, axis=-1, keepdims=True)
    return shifted * (1.0 / total)


def head_rows(ref, block, rows, head):
    values = ref[block * rows : (block + 1) * rows, :]
    low = low_lanes(values.shape)
    return jnp.where(low if head == 0 else jnp.logical_not(low), values, jnp.zeros_like(values))


def attend_kernel(
    at_ref, t0, t1, t2, t3, t4, t5, t6, t7, w0, w1, w2, w3, cos_ref, sin_ref, qgain_ref, kgain_ref,
    normed_ref, raw_ref, query_ref, key_ref, value_ref, mixed_ref, gains_ref, cols_ref, *, rows,
):
    block, dp = at_ref[0], at_ref[1]
    size, width = t0.shape
    thin = width // 32
    gains = jnp.zeros((16, 256), f32)
    for flip, ref in enumerate((w0, w1, w2, w3)):
        for t in range(8):
            cols_ref[aligned((dp ^ flip) * 8 + t, thin), :] = ref[t, 0:thin, :]
            gains += ref[t, thin : thin + 16, :].astype(f32)
    gains_ref[...] = gains
    for slot, ref in enumerate((t0, t1, t2, t3, t4, t5, t6, t7)):
        flip = (slot % 4) * 2 + slot // 4
        values = ref[...].astype(f32)
        scale = lax.rsqrt(jnp.mean(values * values, axis=-1, keepdims=True) + epsilon)
        for j in range(4):
            cut = values[:, j * 256 : (j + 1) * 256] * scale * gains[j : j + 1, :]
            normed_ref[aligned(block ^ flip, size), j * 256 : (j + 1) * 256] = cut.astype(bf16)
    raw_ref[...] = dot(normed_ref[...], cols_ref[...], NN)
    cosine, signed_sine = cos_ref[...], sin_ref[...]
    query = raw_ref[:, 0:128]
    query = query * head_scale(query) * qgain_ref[...]
    query_ref[...] = (query * cosine + halves_swapped(query) * signed_sine).astype(bf16)
    both = raw_ref[:, 128:256]
    low = low_lanes(both.shape)
    value_ref[...] = jnp.where(low, pltpu.roll(both, DH, 1), both).astype(bf16)
    keys = both * head_scale(both) * kgain_ref[...]
    keys = keys * cosine + halves_swapped(keys) * signed_sine
    key_ref[...] = jnp.where(low, keys, pltpu.roll(keys, DH, 1)).astype(bf16)
    for block in range(query_ref.shape[0] // rows):
        end = (block + 1) * rows
        mixed = []
        for head in range(2):
            probs = softmax_block(head_rows(query_ref, block, rows, head), key_ref, block, rows)
            mixed.append(dot(probs.astype(bf16), value_ref[0:end, :], NN))
        chosen = jnp.where(low_lanes(mixed[0].shape), mixed[0], mixed[1]).astype(bf16)
        for i in range(rows // size):
            mixed_ref[block * (rows // size) + i] = chosen[i * size : (i + 1) * size]


def attend_back_kernel(
    grad_ref, query_ref, key_ref, value_ref, raw_ref, cos_ref, sin_ref, qgain_ref, kgain_ref,
    out_ref, terms_ref, gflat, dq_acc, dk_acc, dv_acc, *, rows,
):
    size = grad_ref.shape[1]
    for i in range(grad_ref.shape[0]):
        gflat[i * size : (i + 1) * size, :] = grad_ref[i]
    dk_acc[...] = jnp.zeros_like(dk_acc)
    dv_acc[...] = jnp.zeros_like(dv_acc)
    for block in range(query_ref.shape[0] // rows):
        end = (block + 1) * rows
        grads = []
        for head in range(2):
            query_blk = head_rows(query_ref, block, rows, head)
            probs = softmax_block(query_blk, key_ref, block, rows)
            grad_blk = head_rows(gflat, block, rows, head)
            grad_probs = dot(grad_blk, value_ref[0:end, :], NT)
            delta = jnp.sum(probs * grad_probs, axis=-1, keepdims=True)
            grad_scores = (probs * (grad_probs - delta)).astype(bf16)
            grads.append(dot(grad_scores, key_ref[0:end, :], NN))
            dk_acc[0:end, :] += dot(grad_scores, query_blk, TN)
            dv_acc[0:end, :] += dot(probs.astype(bf16), grad_blk, TN)
        dq_acc[block * rows : end, :] = jnp.where(low_lanes(grads[0].shape), grads[0], grads[1])
    cosine, signed_sine = cos_ref[...], sin_ref[...]

    def through(grad, raw, gain):
        grad = grad.astype(bf16).astype(f32)
        grad = grad * cosine - halves_swapped(grad) * signed_sine
        scale = head_scale(raw)
        normed = raw * scale
        scaled = grad * gain
        inner = scale * (scaled - normed * head_means(scaled * normed))
        return inner, jnp.sum(grad * normed, axis=0, keepdims=True)

    dq, query_terms = through(dq_acc[...] * (DH**-0.5), raw_ref[:, 0:128], qgain_ref[...])
    dk = dk_acc[...]
    dk, key_terms = through((dk + pltpu.roll(dk, DH, 1)) * (DH**-0.5), raw_ref[:, 128:256], kgain_ref[...])
    dv = dv_acc[...]
    dv = dv + pltpu.roll(dv, DH, 1)
    both = jnp.where(low_lanes(dv.shape), dk, dv).astype(bf16)
    dq = dq.astype(bf16)
    for i in range(out_ref.shape[0]):
        out_ref[i, :, 0:128] = dq[i * size : (i + 1) * size]
        out_ref[i, :, 128:256] = both[i * size : (i + 1) * size]
    terms_ref[0:1, :] = query_terms + pltpu.roll(query_terms, DH, 1)
    terms_ref[1:2, :] = key_terms


def place_rows(at_ref, near_ref, far_ref, out_ref):
    y, c, z, x = (at_ref[i] for i in (2, 3, 4, 5))
    thin = near_ref.shape[1]
    for core, ref in ((0, near_ref), (1, far_ref)):
        for i in range(16):
            owner = (((y ^ (i // 8)) * 2 + (c ^ core)) * 4 + (z ^ (i % 4))) * 2 + (x ^ (i // 4 % 2))
            out_ref[aligned(owner, thin), :] = ref[i]


def place_kernel(at_ref, near_ref, far_ref, out_ref):
    place_rows(at_ref, near_ref, far_ref, out_ref)


def middle_kernel(mixed_ref, own_ref, out_weight_ref, gains_ref, attn_ref, middle_ref, normed_ref):
    for h in range(KV):
        attn_ref[:, h * 128 : (h + 1) * 128] = mixed_ref[h]
    middle = own_ref[...].astype(f32) + dot(attn_ref[...], out_weight_ref[...], NN)
    middle_ref[...] = middle
    scale = lax.rsqrt(jnp.mean(middle * middle, axis=-1, keepdims=True) + epsilon)
    for j in range(4):
        cut = middle[:, j * 256 : (j + 1) * 256] * scale * gains_ref[4 + j : 5 + j, :]
        normed_ref[:, j * 256 : (j + 1) * 256] = cut.astype(bf16)


def gain_row(gains, first):
    return jnp.concatenate([gains[first + j : first + j + 1, :] for j in range(4)], axis=1)


def middle_back_kernel(
    sum_ref, r1, r2, r3, middle_ref, grad_ref, out_weight_ref, gains_ref, dm_ref, dmb_ref, dattn_ref
):
    grad = sum_ref[...] + r1[...].astype(f32) + r2[...].astype(f32) + r3[...].astype(f32)
    inner, _ = norm_back(middle_ref[...], gain_row(gains_ref[...], 4), grad)
    dm = grad_ref[...].astype(f32) + inner
    dm_ref[...] = dm
    dmb = dm.astype(bf16)
    dmb_ref[...] = dmb
    dattn = dot(dmb, out_weight_ref[...], NT).astype(bf16)
    for h in range(KV):
        dattn_ref[h] = dattn[:, h * 128 : (h + 1) * 128]


def input_back_kernel(grads_ref, weight_ref, own_ref, gains_ref, dm_ref, out_ref, flat):
    for h in range(KV):
        flat[:, h * 256 : (h + 1) * 256] = grads_ref[h]
    grad = dot(flat[...], weight_ref[...], NT)
    inner, _ = norm_back(own_ref[...].astype(f32), gain_row(gains_ref[...], 0), grad)
    out_ref[...] = dm_ref[...] + inner


def wide_place_kernel(at_ref, g0, g1, g2, g3, d0, d1, d2, d3, gate_ref, up_ref, down_ref):
    y, x = at_ref[2], at_ref[5]
    thin, tall = g0.shape[2], d0.shape[0]
    for flip, (wide, down) in enumerate(((g0, d0), (g1, d1), (g2, d2), (g3, d3))):
        ys, xs = y ^ (flip // 2), x ^ (flip % 2)
        for i in range(8):
            row = aligned((ys * 8 + i) * 2 + xs, thin)
            gate_ref[row, :] = wide[i, 0]
            up_ref[row, :] = wide[i, 1]
        down_ref[aligned(ys * 2 + xs, tall), :] = down[...]


def wide_cut_kernel(at_ref, gate_ref, up_ref, down_ref, *outs):
    y, x = at_ref[2], at_ref[5]
    thin, tall = outs[0].shape[2], outs[4].shape[0]
    for flip in range(4):
        ys, xs = y ^ (flip // 2), x ^ (flip % 2)
        wide, down = outs[flip], outs[4 + flip]
        for i in range(8):
            row = aligned((ys * 8 + i) * 2 + xs, thin)
            wide[i, 0] = gate_ref[row, :].astype(wide.dtype)
            wide[i, 1] = up_ref[row, :].astype(wide.dtype)
        down[...] = down_ref[aligned(ys * 2 + xs, tall), :].astype(down.dtype)


def wide_end_kernel(sums_ref, gate_w_ref, up_w_ref, gain_ref, gate_ref, up_ref, dgain_ref):
    piece = sums_ref.shape[3] // 2
    for y in range(2):
        for owner in range(8):
            start = (y * 8 + owner) * piece
            gate_ref[:, start : start + piece] = sums_ref[owner, 0, :, y * piece : (y + 1) * piece].astype(f32)
            up_ref[:, start : start + piece] = sums_ref[owner, 1, :, y * piece : (y + 1) * piece].astype(f32)
    total = jnp.sum(gate_w_ref[...].astype(f32) * gate_ref[...], axis=-1, keepdims=True)
    total += jnp.sum(up_w_ref[...].astype(f32) * up_ref[...], axis=-1, keepdims=True)
    dgain_ref[...] = total / gain_ref[...]


def thin_end_kernel(sums_ref, rows_ref, gain_ref, query_ref, key_ref, value_ref, dgain_ref):
    total = jnp.zeros_like(dgain_ref)
    for t in range(KV):
        got = sums_ref[t].astype(f32)
        query_ref[:, t * 128 : (t + 1) * 128] = got[:, 0:128]
        key_ref[:, t * DH : (t + 1) * DH] = got[:, 128:192]
        value_ref[:, t * DH : (t + 1) * DH] = got[:, 192:256]
        weight = rows_ref[:, t * 256 : (t + 1) * 256].astype(f32)
        total += jnp.sum(weight * got, axis=-1, keepdims=True)
    dgain_ref[...] = total / gain_ref[...]


def split_device(
    tokens,
    positions,
    d_out,
    first_gain,
    second_gain,
    query_gain,
    key_gain,
    query_weight,
    key_weight,
    value_weight,
    out_weight,
    gate_weight,
    up_weight,
    down_weight,
):
    y, c, z, x = (lax.axis_index(n) for n in AXES)
    at = jnp.stack([z * 2 + x, y * 2 + c, y, c, z, x]).astype(jnp.int32)
    flat_index = ((y * 2 + c) * 4 + z) * 2 + x
    own, grad_own_rows = tokens[0], d_out[0]
    rows, width = own.shape
    length = rows * KV
    thin, hidden = gate_weight.shape
    hid = hidden // 8
    tall = down_weight.shape[0]

    near = [own] + [swap(own, z=k) for k in (1, 2, 3)]
    side = [swap(r, x=1) for r in near]

    lanes = jnp.arange(width, dtype=jnp.int32) // thin == flat_index
    spread = [jnp.where(lanes, jnp.tile(g, width // thin), 0).reshape(4, 256) for g in (first_gain, second_gain)]
    place = positions.astype(jnp.int32)
    place = jnp.concatenate([place // 32, place % 32], axis=1).astype(bf16)
    extra = jnp.concatenate(spread + [place, jnp.zeros((7, 256), bf16)])
    wide_cut, cols_cut, qkv_rows = kernel_call(
        cut_kernel,
        [shape((8, 2, thin, hid), bf16), shape((KV, thin + 16, 256), bf16), shape((thin, KV * 256), bf16)],
        gate_weight, up_weight, query_weight, key_weight, value_weight, extra, name="cut",
    )
    cols = [to_all(cols_cut, ("z", "x"))]
    cols.append(swap(cols[0], c=1))
    cols += [swap(p, y=1) for p in cols]
    place = cols[0][:, thin + 8, :].astype(f32)
    pos_seq = (place[:, :128] * 32 + place[:, 128:]).reshape(length)
    cosine, sine_part = (t[:, 0] for t in rope_tables(pos_seq))
    cosine = jnp.tile(cosine, (1, 4))
    signed_sine = jnp.tile(jnp.concatenate([-sine_part, sine_part], axis=1), (1, 2))

    def all_rows(weight):
        stacked = jnp.stack([weight] + [swap(weight, z=k) for k in (1, 2, 3)])
        stacked = jnp.concatenate([stacked, swap(stacked, x=1)])
        stacked = jnp.concatenate([stacked, swap(stacked, y=1)])
        return kernel_call(
            place_kernel, [shape((32 * thin, weight.shape[1]), bf16)], stacked, swap(stacked, c=1),
            name="place", scalars=at,
        )[0]

    out_full = all_rows(out_weight)

    def around(value):
        return [swap(value, x=1), swap(value, y=1), swap(value, y=1, x=1)]

    down_parts = [down_weight] + around(down_weight)
    wide_own = to_all(wide_cut, ("c", "z"))
    wide_parts = [wide_own] + around(wide_own)
    gate_full, up_full, down_full = kernel_call(
        wide_place_kernel,
        [shape((width, hid), bf16), shape((width, hid), bf16), shape((hid, width), bf16)],
        *wide_parts, *down_parts, name="wide_place", scalars=at,
    )

    qgain = jnp.tile(query_gain.astype(f32), 2).reshape(1, 128)
    kgain = jnp.tile(key_gain.astype(f32), 2).reshape(1, 128)
    work = 2 * length * length * DH
    lane = shape((length, 128), bf16)
    normed_seq, raw, query_bf, key_bf, value_bf, mixed, gains = kernel_call(
        lambda *refs: attend_kernel(*refs, rows=256),
        [shape((length, width), bf16), shape((length, 256), f32), lane, lane, lane,
         shape((KV, rows, 128), bf16), shape((16, 256), f32)],
        *near, *side, *cols, cosine, signed_sine, qgain, kgain,
        scratch=[pltpu.VMEM((width, 256), bf16)], flops=4 * work + 2 * length * width * 256,
        transcendentals=2 * length * length, name="attend", scalars=at,
    )
    mixed = to_all(mixed, ("z", "x"))
    attn_bf, middle, normed_two = kernel_call(
        middle_kernel,
        [shape((rows, width), bf16), shape((rows, width), f32), shape((rows, width), bf16)],
        mixed, own, out_full, gains, flops=2 * rows * width * width, name="middle",
    )

    def gather_slots(value):
        near = [value] + [swap(value, z=k) for k in (1, 2, 3)]
        return jnp.concatenate(near + [swap(r, c=1) for r in near])

    def core_sum(partial):
        half = partial.shape[0] // 2
        return partial[:half] + swap(partial[half:].astype(bf16), c=1).astype(f32)

    def line_parts(kept):
        return [swap(kept[k * rows : (k + 1) * rows].astype(bf16), z=k) for k in (1, 2, 3)]

    grad_slots = gather_slots(after(grad_own_rows, near[1], near[2], near[3]))
    slots = gather_slots(normed_two)
    gate_pre = dot(slots, gate_full, NN)
    up_pre = dot(slots, up_full, NN)
    sigmoid_gate = jax.nn.sigmoid(gate_pre)
    hidden_bf = (gate_pre * sigmoid_gate * up_pre).astype(bf16)
    grad_hidden = dot(grad_slots, down_full, NT)
    grad_gate = (
        grad_hidden * up_pre * sigmoid_gate * (1.0 + gate_pre * (1.0 - sigmoid_gate))
    ).astype(bf16)
    grad_up = (grad_hidden * gate_pre * sigmoid_gate).astype(bf16)
    kept = core_sum(dot(grad_gate, gate_full, NT) + dot(grad_up, up_full, NT))
    parts = line_parts(kept)
    dm, grad_mid_bf, grad_attn = kernel_call(
        middle_back_kernel,
        [shape((rows, width), f32), shape((rows, width), bf16), shape((KV, rows, 128), bf16)],
        kept[:rows], *parts, middle, grad_own_rows, out_full, gains,
        flops=2 * rows * width * width, name="middle_back",
    )
    grad_attn = to_all(grad_attn, ("z", "x"))

    hidden_late, gate_late, up_late = (after(v, kept) for v in (hidden_bf, grad_gate, grad_up))
    cuts = kernel_call(
        wide_cut_kernel,
        [shape((8, 2, thin, hid), f32 if i == 0 else bf16) for i in range(4)]
        + [shape((tall, width), f32 if i == 0 else bf16) for i in range(4)],
        dot(slots, gate_late, TN), dot(slots, up_late, TN), dot(hidden_late, grad_slots, TN),
        name="wide_cut", scalars=at,
    )

    def back_around(values):
        return [swap(values[1], x=1), swap(values[2], y=1), swap(values[3], y=1, x=1)]

    wide_back, down_back = back_around(cuts[:4]), back_around(cuts[4:])
    out_kept = core_sum(dot(hidden_late, down_full, NN))
    out_parts = line_parts(after(out_kept, *parts))

    back_work = 5 * work
    grad_qkv, head_terms = kernel_call(
        lambda *refs: attend_back_kernel(*refs, rows=256),
        [shape((KV, rows, 256), bf16), shape((2, 128), f32)],
        grad_attn, query_bf, key_bf, value_bf, raw, cosine, signed_sine, qgain, kgain,
        scratch=[pltpu.VMEM((length, 128), bf16)] + [pltpu.VMEM((length, 128), f32)] * 3,
        flops=2 * back_work, transcendentals=2 * length * length, name="attend_back",
    )
    grad_own = to_all(grad_qkv, ("z", "x"))
    head_sums = head_terms
    for flips in ({"c": 1}, {"x": 1}, {"z": 1}, {"z": 2}, {"y": 1}):
        head_sums = head_sums + swap(head_sums, **flips)
    grad_qkv_w = dot(normed_seq, grad_qkv.reshape(length, 256), TN).reshape(2, 2, width // 4, 256)
    grad_qkv_w = part(grad_qkv_w, 1, c) + swap(part(grad_qkv_w, 1, 1 - c), c=1)
    grad_qkv_w = part(grad_qkv_w, 0, y) + swap(part(grad_qkv_w, 0, 1 - y), y=1)
    grad_qkv_w = to_all(grad_qkv_w.reshape(KV, thin, 256), ("z", "x"))

    qkv_full = all_rows(after(qkv_rows, slots))
    (d_tokens,) = kernel_call(
        input_back_kernel, [shape((rows, width), f32)],
        grad_own, qkv_full, own, gains, dm,
        scratch=[pltpu.VMEM((rows, KV * 256), bf16)], flops=4 * rows * width * width, name="input_back",
    )

    grad_out_w = dot(attn_bf, after(grad_mid_bf, grad_attn), TN).reshape(2, 2, 4, 2, thin, width)

    def halve(value, axis, at, **flips):
        sent = part(value, axis, 1 - at).astype(bf16)
        return part(value, axis, at) + swap(sent, **flips).astype(f32)

    grad_out_w = halve(grad_out_w, 1, c, c=1)
    grad_out_w = halve(grad_out_w, 0, y, y=1)
    grad_out_w = halve(grad_out_w, 1, x, x=1)
    total = part(grad_out_w, 0, z)
    for k in (1, 2, 3):
        total = total + swap(part(grad_out_w, 0, z ^ k).astype(bf16), z=k).astype(f32)
    grad_out_w = total

    output = middle + out_kept[:rows] + sum(p.astype(f32) for p in out_parts)
    grad_down_w = cuts[4] + sum(p.astype(f32) for p in down_back)
    grad_wide = cuts[0] + sum(p.astype(f32) for p in wide_back)
    grad_wide = to_all(grad_wide, ("c", "z"))
    grad_gate_w, grad_up_w, second_gain_grad = kernel_call(
        wide_end_kernel,
        [shape((thin, hidden), f32), shape((thin, hidden), f32), shape((thin, 1), f32)],
        grad_wide, gate_weight, up_weight, second_gain.astype(f32)[:, None], name="wide_end",
    )
    grad_query_w, grad_key_w, grad_value_w, first_gain_grad = kernel_call(
        thin_end_kernel,
        [shape((thin, width), f32), shape((thin, width // 2), f32), shape((thin, width // 2), f32),
         shape((thin, 1), f32)],
        grad_qkv_w, qkv_rows, first_gain.astype(f32)[:, None], name="thin_end",
    )
    return (
        output.astype(bf16)[None],
        d_tokens[None],
        first_gain_grad[:, 0],
        second_gain_grad[:, 0],
        head_sums[0, :DH],
        head_sums[1, :DH],
        grad_query_w,
        grad_key_w,
        grad_value_w,
        grad_out_w,
        grad_gate_w,
        grad_up_w,
        grad_down_w,
    )


def split_solution(mesh):
    inner = Mesh(mesh.devices.reshape([SIZES[n] for n in AXES]), AXES)
    every, dp, ctx = AXES, ("y", "c"), ("z", "x")
    seq, vec, mat = P(dp, ctx, None), P(every), P(every, None)
    return jax.shard_map(
        split_device,
        mesh=inner,
        in_specs=(seq, P(dp, ctx), seq, vec, vec, P(), P()) + (mat,) * 7,
        out_specs=(seq, seq, vec, vec, P(), P()) + (mat,) * 7,
        check_vma=False,
    )


def solution(mesh):
    if mesh.shape["dp"] == 4 and mesh.shape["ctx"] == KV:
        return split_solution(mesh)
    in_specs = (
        P("dp", "ctx", None),
        P("dp", "ctx"),
        P("dp", "ctx", None),
        P(("dp", "ctx")),
        P(("dp", "ctx")),
        P(),
        P(),
        P(("dp", "ctx"), None),
        P(("dp", "ctx"), None),
        P(("dp", "ctx"), None),
        P(("dp", "ctx"), None),
        P(("dp", "ctx"), None),
        P(("dp", "ctx"), None),
        P(("dp", "ctx"), None),
    )
    out_specs = (
        P("dp", "ctx", None),
        P("dp", "ctx", None),
        P(("dp", "ctx")),
        P(("dp", "ctx")),
        P(),
        P(),
        P(("dp", "ctx"), None),
        P(("dp", "ctx"), None),
        P(("dp", "ctx"), None),
        P(("dp", "ctx"), None),
        P(("dp", "ctx"), None),
        P(("dp", "ctx"), None),
        P(("dp", "ctx"), None),
    )
    return jax.shard_map(
        generic_device, mesh=mesh, in_specs=in_specs, out_specs=out_specs, check_vma=False
    )
```
